32 devices in a mesh: tile: 8 (over y, x, core), frame: 4 (over z).
Axes of the slice: x: 2, y: 2, z: 4, core: 2. Of those that a mesh axis runs over, the one named last changes fastest.
Arguments:
- object_slices: float32 [2, 2, 2048, 1024], P(None, None, 'tile', 'frame'), may hold values from -6 to 6
- probe_modes: float32 [2, 2, 256, 256], replicated, may hold values from -3 to 3
- prop_phase: float32 [256, 256], replicated, may hold values from -3.140625 to 3.140625
- background: float32 [256, 256], replicated, may hold values from 0.1 to 1
- positions: int32 [64, 2], P(('tile', 'frame')), may hold values from 0 to 768, as said below
- counts: int32 [64, 256, 256], P(('tile', 'frame')), may hold values from 0 to 8
Outputs:
- object_grad: float32 [2, 2, 2048, 1024], P(None, None, 'tile', 'frame')
- probe_grad: float32 [2, 2, 256, 256], replicated
The draws below stay inside these ranges and needn't reach their ends.
Inputs may be any that keep to these rules, and one draw needn't show every extreme that they name: `positions`: rows lie in 0 to 256, columns in 0 to 768.
All inputs are finite; a program needn't handle non-finite values.
Results may differ from the reference program's by a relative error of at most 0.0003.
Values sent between devices are 32-bit elements; how exact they have to be, the bound alone decides.
No kernel may reach another device: no remote copies, remote signals or barrier semaphores. Data moves between devices by JAX's collectives and lax.ppermute only.
A program may use at most 128 MiB of HBM per device.

```python
import math
import jax
import jax.numpy as jnp
from jax import lax

FRAME = 256
MODES = 2
SLICES = 2
TILE_ROWS = 256
COLS = 1024
HALO = 128
F_DEV = 2
NROWS = 2048
FRAMES = 64
N_FRAME = 4


def draw_positions(key, part):
    first_key, second_key = jax.random.split(jax.random.fold_in(key, 17))
    rows_drawn = jax.random.randint(first_key, (FRAMES,), 0, TILE_ROWS + 2 * HALO - FRAME + 1)
    cols_drawn = jax.random.randint(second_key, (FRAMES,), 0, COLS - FRAME + 1)
    return jnp.stack([rows_drawn, cols_drawn], axis=1).astype(jnp.int32)


def set_ends(entries, rng, low, top_value):
    longest = entries.shape.index(max(entries.shape))
    spots = []
    for shift in (0, 1):
        where = [jax.random.randint(jax.random.fold_in(rng, axis), (), 0, length) for axis, length in enumerate(entries.shape)]
        where[longest] = (where[longest] + shift) % entries.shape[longest]
        spots.append(tuple(where))
    return entries.at[spots[0]].set(low).at[spots[1]].set(top_value)


def block_scale(rng, shape, cuts, low, top_value):
    def one(axis_at, shards_of):
        heights = jax.random.uniform(jax.random.fold_in(jax.random.fold_in(rng, 6), axis_at), (shards_of,), jnp.float32, low / len(cuts), top_value / len(cuts))
        return jnp.repeat(jnp.exp(heights), shape[axis_at] // shards_of).reshape((-1,) + (1,) * (len(shape) - axis_at - 1))

    loudness = one(*cuts[0])
    for cut in cuts[1:]:
        loudness = loudness * one(*cut)
    return loudness


def bell_draw(stream_key, shape, width, reach, cuts=(), kind=jnp.bfloat16):
    drawn = jax.random.normal(stream_key, shape, jnp.float32) * width
    if len(cuts) > 0:
        drawn = block_scale(stream_key, shape, cuts, -0.22, 0.18) * drawn
    return jnp.clip(drawn, min=-reach, max=reach).astype(kind)


def setup_inputs(seed: int = 0) -> dict:
    streams_of = jax.random.split(jax.random.key(seed), 7)
    object_slices = bell_draw(streams_of[0], (SLICES, 2, NROWS, COLS), 1.0, 6.0, ((2, 8), (3, 4)), jnp.float32)
    probe_modes = bell_draw(streams_of[1], (MODES, 2, FRAME, FRAME), 0.35, 3.0, (), jnp.float32)
    prop_phase = jnp.clip(jax.random.uniform(streams_of[2], (FRAME, FRAME), jnp.float32, -3.140625, 3.140625), -3.140625, 3.140625)
    background = jnp.clip(jnp.exp(jax.random.uniform(streams_of[3], (FRAME, FRAME), jnp.float32, math.log(0.1), math.log(1.0))), 0.1, 1.0)
    positions = draw_positions(jax.random.fold_in(streams_of[6], 71), 0)
    counts = set_ends(jax.random.randint(streams_of[5], (FRAMES, FRAME, FRAME), 0, 9), jax.random.fold_in(streams_of[5], 1), 0, 8).astype(jnp.int32)
    return dict(object_slices=object_slices, probe_modes=probe_modes, prop_phase=prop_phase, background=background, positions=positions, counts=counts)


def matmul_high(left, right):
    return jnp.matmul(left, right, precision=lax.Precision.HIGHEST)


def dft_tables(length):
    index = jnp.arange(length, dtype=jnp.int32)
    product = (index[:, None] * index[None, :]) % length
    angles = product.astype(jnp.float32) * (-2.0 * 3.141592653589793 / length)
    scale = length ** -0.5
    return jnp.cos(angles) * scale, jnp.sin(angles) * scale


def transform(wave_re, wave_im, table_re, table_im):
    left_re = matmul_high(table_re, wave_re) - matmul_high(table_im, wave_im)
    left_im = matmul_high(table_re, wave_im) + matmul_high(table_im, wave_re)
    out_re = matmul_high(left_re, table_re) - matmul_high(left_im, table_im)
    out_im = matmul_high(left_re, table_im) + matmul_high(left_im, table_re)
    return out_re, out_im


def propagate(wave_re, wave_im, kern_re, kern_im, table_re, table_im):
    spec_re, spec_im = transform(wave_re, wave_im, table_re, table_im)
    spec_re, spec_im = spec_re * kern_re - spec_im * kern_im, spec_re * kern_im + spec_im * kern_re
    return transform(spec_re, spec_im, table_re, -table_im)


def frame_gradients(windows, probe_modes, prop_phase, background, measured, tables):
    table_re, table_im = tables
    batch_size = windows.shape[0]
    slice_count = windows.shape[1]
    mode_count = probe_modes.shape[0]
    length = probe_modes.shape[-1]
    kern_re = jnp.cos(prop_phase)
    kern_im = jnp.sin(prop_phase)
    wave_re = jnp.broadcast_to(probe_modes[:, 0][None], (batch_size, mode_count, length, length))
    wave_im = jnp.broadcast_to(probe_modes[:, 1][None], (batch_size, mode_count, length, length))
    incoming = []
    for layer_index in range(slice_count):
        obj_re = windows[:, layer_index, 0][:, None]
        obj_im = windows[:, layer_index, 1][:, None]
        incoming.append((wave_re, wave_im))
        wave_re, wave_im = wave_re * obj_re - wave_im * obj_im, wave_re * obj_im + wave_im * obj_re
        if layer_index < slice_count - 1:
            wave_re, wave_im = propagate(wave_re, wave_im, kern_re, kern_im, table_re, table_im)
    far_re, far_im = transform(wave_re, wave_im, table_re, table_im)
    intensity = jnp.sum(far_re * far_re + far_im * far_im, axis=1) + background
    weight = (1.0 - measured / intensity)[:, None]
    back_re, back_im = transform(weight * far_re, weight * far_im, table_re, -table_im)
    slice_terms = [None] * slice_count
    for layer_index in reversed(range(slice_count)):
        before_re, before_im = incoming[layer_index]
        obj_re = windows[:, layer_index, 0][:, None]
        obj_im = windows[:, layer_index, 1][:, None]
        grad_re = jnp.sum(before_re * back_re + before_im * back_im, axis=1)
        grad_im = jnp.sum(before_re * back_im - before_im * back_re, axis=1)
        slice_terms[layer_index] = jnp.stack([grad_re, grad_im], axis=1)
        back_re, back_im = back_re * obj_re + back_im * obj_im, back_im * obj_re - back_re * obj_im
        if layer_index > 0:
            back_re, back_im = propagate(back_re, back_im, kern_re, -kern_im, table_re, table_im)
    probe_term = jnp.sum(jnp.stack([back_re, back_im], axis=2), axis=0)
    return jnp.stack(slice_terms, axis=1), probe_term


def reference(object_slices, probe_modes, prop_phase, background, positions, counts):
    rows_all = object_slices.shape[2]
    padded = jnp.concatenate([object_slices[:, :, rows_all - HALO:], object_slices, object_slices[:, :, :HALO]], axis=2)
    tables = dft_tables(FRAME)
    per_tile = N_FRAME * F_DEV

    def advance(running, frame_item):
        grad_acc, probe_acc = running
        frame_place, measured, number = frame_item
        tile_index = number // per_tile
        zero_index = jnp.zeros((), jnp.int32)
        start_index = (zero_index, zero_index, (tile_index * TILE_ROWS + frame_place[0]).astype(jnp.int32), frame_place[1].astype(jnp.int32))
        window = lax.dynamic_slice(padded, start_index, (SLICES, 2, FRAME, FRAME))
        slice_terms, probe_term = frame_gradients(window[None], probe_modes, prop_phase, background, measured.astype(jnp.float32)[None], tables)
        current = lax.dynamic_slice(grad_acc, start_index, (SLICES, 2, FRAME, FRAME))
        grad_acc = lax.dynamic_update_slice(grad_acc, current + slice_terms[0], start_index)
        return (grad_acc, probe_acc + probe_term), None

    initial = (jnp.zeros(padded.shape, jnp.float32), jnp.zeros(probe_modes.shape, jnp.float32))
    numbers = jnp.arange(positions.shape[0], dtype=jnp.int32)
    (grad_acc, probe_grad), unused = lax.scan(advance, initial, (positions, counts, numbers))
    object_grad = grad_acc[:, :, HALO:HALO + rows_all]
    object_grad = object_grad.at[:, :, rows_all - HALO:].add(grad_acc[:, :, :HALO])
    object_grad = object_grad.at[:, :, :HALO].add(grad_acc[:, :, HALO + rows_all:])
    return object_grad, probe_grad
```

```python
import functools

import jax
import jax.numpy as jnp
from jax import lax
from jax.experimental import pallas as pl
from jax.experimental.pallas import tpu as pltpu
from jax.sharding import PartitionSpec as P

HALO = 128
F32 = jnp.float32
BF16 = jnp.bfloat16
ROW_PAD = 8
COL_PAD = 128
VMEM_LIMIT = 60 * 1024 * 1024


def dft_blocks(length):
    half = length // 2
    row = lax.broadcasted_iota(jnp.int32, (half, half), 0)
    col = lax.broadcasted_iota(jnp.int32, (half, half), 1)
    tables = []
    for odd in (0, 1):
        product = (col * (2 * row + odd)) % length
        angles = product.astype(F32) * (-2.0 * 3.141592653589793 / length)
        scale = length ** (-0.5)
        re, im = jnp.cos(angles) * scale, jnp.sin(angles) * scale
        forward = jnp.concatenate(
            [jnp.concatenate([re, -im], axis=1), jnp.concatenate([im, re], axis=1)], axis=0
        )
        tables.append(forward)
    return tables


def two_terms(matrix):
    high = matrix.astype(BF16)
    low = (matrix - high.astype(F32)).astype(BF16)
    return high, low


def table_terms(matrix):
    high = lax.reduce_precision(matrix, 8, 7)
    return high.astype(BF16), (matrix - high).astype(BF16)


def left_table(matrix):
    high, low = table_terms(matrix)
    return jnp.concatenate([high, low, high], axis=1)


def right_table(matrix):
    high, low = table_terms(matrix)
    return jnp.concatenate([high, low, high], axis=0)


def dot(left, right):
    return lax.dot_general(left, right, (((1,), (0,)), ((), ())), preferred_element_type=F32)


def stack_terms(value, axis):
    high, low = two_terms(value)
    return jnp.concatenate([high, high, low], axis=axis)


def left_forward(re, im, tables):
    half = re.shape[0] // 2
    outs = []
    for sign, table in zip((1, -1), tables):
        if sign > 0:
            parts = [re[:half] + re[half:], im[:half] + im[half:]]
        else:
            parts = [re[:half] - re[half:], im[:half] - im[half:]]
        outs.append(dot(table[...], stack_terms(jnp.concatenate(parts, axis=0), 0)))
    even, odd = outs
    return (
        jnp.concatenate([even[:half], odd[:half]], axis=0),
        jnp.concatenate([even[half:], odd[half:]], axis=0),
    )


def right_forward(re, im, tables):
    half = re.shape[1] // 2
    outs = []
    for sign, table in zip((1, -1), tables):
        if sign > 0:
            parts = [re[:, :half] + re[:, half:], im[:, :half] + im[:, half:]]
        else:
            parts = [re[:, :half] - re[:, half:], im[:, :half] - im[:, half:]]
        outs.append(dot(stack_terms(jnp.concatenate(parts, axis=1), 1), table[...]))
    even, odd = outs
    return (
        jnp.concatenate([even[:, :half], odd[:, :half]], axis=1),
        jnp.concatenate([even[:, half:], odd[:, half:]], axis=1),
    )


def right_inverse(re, im, tables):
    half = re.shape[1] // 2
    even = dot(stack_terms(jnp.concatenate([re[:, :half], im[:, :half]], axis=1), 1), tables[0][...])
    odd = dot(stack_terms(jnp.concatenate([re[:, half:], im[:, half:]], axis=1), 1), tables[1][...])
    first, second = even + odd, even - odd
    return (
        jnp.concatenate([first[:, :half], second[:, :half]], axis=1),
        jnp.concatenate([first[:, half:], second[:, half:]], axis=1),
    )


def left_inverse(re, im, tables):
    half = re.shape[0] // 2
    even = dot(tables[0][...], stack_terms(jnp.concatenate([re[:half], im[:half]], axis=0), 0))
    odd = dot(tables[1][...], stack_terms(jnp.concatenate([re[half:], im[half:]], axis=0), 0))
    first, second = even + odd, even - odd
    return (
        jnp.concatenate([first[:half], second[:half]], axis=0),
        jnp.concatenate([first[half:], second[half:]], axis=0),
    )


def forward(re, im, tabs):
    return right_forward(*left_forward(re, im, tabs[0:2]), tabs[4:6])


def inverse(re, im, tabs):
    return left_inverse(*right_inverse(re, im, tabs[6:8]), tabs[2:4])


def place_of(pos_ref, frame, rows, cols, length):
    row, col = pos_ref[frame, 0], pos_ref[frame, 1]
    row_at = jnp.minimum((row // ROW_PAD) * ROW_PAD, rows - length - ROW_PAD)
    col_at = jnp.minimum((col // COL_PAD) * COL_PAD, cols - length - COL_PAD)
    return (
        pl.multiple_of(row_at, ROW_PAD),
        pl.multiple_of(col_at, COL_PAD),
        row - row_at,
        col - col_at,
    )


def take_window(ext, plane, place, length):
    row_at, col_at, row_by, col_by = place
    tall, wide = length + ROW_PAD, length + COL_PAD
    block = ext[plane, pl.ds(row_at, tall), pl.ds(col_at, wide)]
    block = pltpu.roll(block, (wide - col_by) % wide, 1)[:, :length]
    return pltpu.roll(block, (tall - row_by) % tall, 0)[:length]


def add_window(acc, plane, place, value):
    row_at, col_at, row_by, col_by = place
    length = value.shape[0]
    block = jnp.concatenate([value, jnp.zeros((ROW_PAD, length), F32)], axis=0)
    block = pltpu.roll(block, row_by, 0)
    block = jnp.concatenate([block, jnp.zeros((length + ROW_PAD, COL_PAD), F32)], axis=1)
    block = pltpu.roll(block, col_by, 1)
    rows, cols = pl.ds(row_at, length + ROW_PAD), pl.ds(col_at, length + COL_PAD)
    acc[plane, rows, cols] = acc[plane, rows, cols] + block


def strip_column(side, order, strips, width):
    half = strips // 2
    if order < half:
        low, high = half - 1 - order, half + order
    else:
        low, high = order, strips - 1 - order
    return pl.multiple_of(jnp.where(side == 0, low, high) * width, width)


def load_strips(side, strips, above, below, ext, sem):
    count = len(strips)
    copies = []
    for order in range(count):
        tall, width = strips[order].shape[1:]
        halo = above[order].shape[1]
        cols = pl.ds(strip_column(side, order, count, width), width)
        for part, first, high in ((above, 0, halo), (strips, halo, tall), (below, halo + tall, halo)):
            copies.append(
                pltpu.make_async_copy(part[order], ext.at[:, pl.ds(first, high), cols], sem.at[len(copies)])
            )
    for copy in copies:
        copy.start()
    for copy in copies:
        copy.wait()


def store_strips(side, acc, core, above, below, sem):
    count, _, tall, width = core.shape
    halo = above.shape[2]
    copies = []
    for order in range(count):
        cols = pl.ds(strip_column(side, order, count, width), width)
        for part, first, high in ((above, 0, halo), (core, halo, tall), (below, halo + tall, halo)):
            copies.append(
                pltpu.make_async_copy(acc.at[:, pl.ds(first, high), cols], part.at[order], sem.at[len(copies)])
            )
    for copy in copies:
        copy.start()
    for copy in copies:
        copy.wait()


def forward_kernel(strips, modes, pos, side, *refs):
    parts, refs = refs[: 3 * strips], refs[3 * strips :]
    probe, kern, refs = refs[0], refs[1], refs[2:]
    tabs, refs = refs[:8], refs[8:]
    wave_out, window_out, ext, sem = refs
    length = probe.shape[-1]
    frame = pl.program_id(0)

    @pl.when(frame == 0)
    def _():
        load_strips(side[0], parts[:strips], parts[strips : 2 * strips], parts[2 * strips :], ext, sem)

    place = place_of(pos, frame, ext.shape[1], ext.shape[2], length)
    for plane in range(2):
        window_out[0, plane] = take_window(ext, plane, place, length)

    def mode_step(mode, carry):
        obj_re, obj_im = window_out[0, 0], window_out[0, 1]
        wave_re, wave_im = probe[mode, 0], probe[mode, 1]
        re = wave_re * obj_re - wave_im * obj_im
        im = wave_re * obj_im + wave_im * obj_re
        re, im = forward(re, im, tabs)
        kern_re, kern_im = kern[0], kern[1]
        re, im = re * kern_re - im * kern_im, re * kern_im + im * kern_re
        re, im = inverse(re, im, tabs)
        wave_out[0, mode, 0] = re
        wave_out[0, mode, 1] = im
        return carry

    lax.fori_loop(0, modes, mode_step, 0)


def middle_kernel(strips, modes, pos, side, *refs):
    parts, refs = refs[: 3 * strips], refs[3 * strips :]
    wave_in, background, counts, refs = refs[0], refs[1], refs[2], refs[3:]
    tabs, refs = refs[:8], refs[8:]
    back_out, core, above, below, refs = refs[0], refs[1], refs[2], refs[3], refs[4:]
    ext, acc, window, far, grad, level, sem = refs
    length = background.shape[-1]
    frame = pl.program_id(0)

    @pl.when(frame == 0)
    def _():
        load_strips(side[0], parts[:strips], parts[strips : 2 * strips], parts[2 * strips :], ext, sem)
        acc[...] = jnp.zeros_like(acc)

    place = place_of(pos, frame, ext.shape[1], ext.shape[2], length)
    for plane in range(2):
        window[plane] = take_window(ext, plane, place, length)
    level[...] = background[...]
    grad[...] = jnp.zeros_like(grad)

    def mode_forward(mode, carry):
        obj_re, obj_im = window[0], window[1]
        wave_re, wave_im = wave_in[0, mode, 0], wave_in[0, mode, 1]
        re = wave_re * obj_re - wave_im * obj_im
        im = wave_re * obj_im + wave_im * obj_re
        re, im = forward(re, im, tabs)
        far[mode, 0] = re
        far[mode, 1] = im
        level[...] = level[...] + (re * re + im * im)
        return carry

    lax.fori_loop(0, modes, mode_forward, 0)
    level[...] = 1.0 - counts[0] / level[...]

    def mode_back(mode, carry):
        weight = level[...]
        re, im = inverse(weight * far[mode, 0], weight * far[mode, 1], tabs)
        wave_re, wave_im = wave_in[0, mode, 0], wave_in[0, mode, 1]
        grad[0] = grad[0] + (wave_re * re + wave_im * im)
        grad[1] = grad[1] + (wave_re * im - wave_im * re)
        obj_re, obj_im = window[0], window[1]
        back_out[0, mode, 0] = re * obj_re + im * obj_im
        back_out[0, mode, 1] = im * obj_re - re * obj_im
        return carry

    lax.fori_loop(0, modes, mode_back, 0)
    for plane in range(2):
        add_window(acc, plane, place, grad[plane])

    @pl.when(frame == pl.num_programs(0) - 1)
    def _():
        store_strips(side[0], acc, core, above, below, sem)


def backward_kernel(strips, modes, pos, side, *refs):
    back_in, window, probe, kern, refs = refs[0], refs[1], refs[2], refs[3], refs[4:]
    tabs, refs = refs[:8], refs[8:]
    term_out, core, above, below, refs = refs[0], refs[1], refs[2], refs[3], refs[4:]
    acc, grad, sem = refs
    length = probe.shape[-1]
    frame = pl.program_id(0)

    @pl.when(frame == 0)
    def _():
        acc[...] = jnp.zeros_like(acc)
        term_out[...] = jnp.zeros_like(term_out)

    place = place_of(pos, frame, acc.shape[1], acc.shape[2], length)
    grad[...] = jnp.zeros_like(grad)

    def mode_step(mode, carry):
        re, im = forward(back_in[0, mode, 0], back_in[0, mode, 1], tabs)
        kern_re, kern_im = kern[0], kern[1]
        re, im = re * kern_re + im * kern_im, im * kern_re - re * kern_im
        re, im = inverse(re, im, tabs)
        wave_re, wave_im = probe[mode, 0], probe[mode, 1]
        grad[0] = grad[0] + (wave_re * re + wave_im * im)
        grad[1] = grad[1] + (wave_re * im - wave_im * re)
        obj_re, obj_im = window[0, 0], window[0, 1]
        term_out[mode, 0] = term_out[mode, 0] + (re * obj_re + im * obj_im)
        term_out[mode, 1] = term_out[mode, 1] + (im * obj_re - re * obj_im)
        return carry

    lax.fori_loop(0, modes, mode_step, 0)
    for plane in range(2):
        add_window(acc, plane, place, grad[plane])

    @pl.when(frame == pl.num_programs(0) - 1)
    def _():
        store_strips(side[0], acc, core, above, below, sem)


def tile_shift(array, by):
    count = lax.axis_size("tile")
    return lax.ppermute(array, "tile", [(i, (i + by) % count) for i in range(count)])


def tile_swap(array, bit):
    count = lax.axis_size("tile")
    return lax.ppermute(array, "tile", [(i, i ^ bit) for i in range(count)])


def shards(object_slices, probe_modes, prop_phase, background, positions, counts):
    strips = lax.axis_size("frame")
    half = strips // 2
    low, high = half - 1, half
    place = lax.axis_index("frame")
    side = (place >= half).astype(jnp.int32).reshape(1)
    slices, _, rows, width = object_slices.shape
    modes, length = probe_modes.shape[0], probe_modes.shape[-1]
    cols = strips * width
    tall = rows + 2 * HALO

    def inward(array):
        return [array] + [
            lax.ppermute(array, "frame", [(low - k, low), (high + k, high)]) for k in range(1, half)
        ]

    def across(array):
        return lax.ppermute(array, "frame", [(low, high), (high, low)])

    def gathered(array):
        own = inward(array)
        every = own + [across(strip) for strip in own]
        above = [tile_shift(strip[:, rows - HALO :], 1) for strip in every]
        below = [tile_shift(strip[:, :HALO], -1) for strip in every]
        return every + above + below

    index = jnp.arange(length, dtype=jnp.int32)
    order = jnp.where(index < length // 2, 2 * index, 2 * index - length + 1)
    pick = (order[:, None] == index[None, :]).astype(F32)

    def sorted_frequencies(array):
        exact = functools.partial(jnp.matmul, precision=lax.Precision.HIGHEST)
        return exact(exact(pick, array), pick.T)

    kern = sorted_frequencies(prop_phase)
    kern = jnp.stack([jnp.cos(kern), jnp.sin(kern)])
    level = sorted_frequencies(background)
    fronts = dft_blocks(length)
    backs = [table.T for table in fronts]
    tabs = (
        [left_table(t) for t in fronts]
        + [left_table(t) for t in backs]
        + [right_table(t) for t in backs]
        + [right_table(t) for t in fronts]
    )

    all_positions = jnp.concatenate(inward(positions), axis=0)
    first = gathered(object_slices[0])
    measured = sorted_frequencies(counts.astype(F32))
    measured = jnp.concatenate(inward(measured), axis=0)
    second = gathered(object_slices[1])
    frames = all_positions.shape[0]

    any_spec = pl.BlockSpec(memory_space=pl.ANY)
    smem_spec = pl.BlockSpec(memory_space=pltpu.SMEM)

    def whole(array):
        shape = array.shape
        return pl.BlockSpec(shape, lambda i: (0,) * len(shape))

    def per_frame(*shape):
        return pl.BlockSpec((1,) + shape, lambda i: (i,) + (0,) * len(shape))

    wave_shape = (modes, 2, length, length)
    pair_shape = (2, length, length)
    sems = pltpu.SemaphoreType.DMA((3 * strips,))
    ext = pltpu.VMEM((2, tall, cols), F32)
    params = pltpu.CompilerParams(dimension_semantics=("arbitrary",), vmem_limit_bytes=VMEM_LIMIT)
    cost = pl.CostEstimate(
        flops=frames * modes * 2 * 12 * 2 * length**3,
        bytes_accessed=4 * (frames * modes * 2 * length * length + 2 * tall * cols),
        transcendentals=0,
    )
    grads_out = [
        jax.ShapeDtypeStruct((strips, 2, rows, width), F32),
        jax.ShapeDtypeStruct((strips, 2, HALO, width), F32),
        jax.ShapeDtypeStruct((strips, 2, HALO, width), F32),
    ]
    tab_specs = [whole(t) for t in tabs]

    waves, windows = pl.pallas_call(
        functools.partial(forward_kernel, strips, modes),
        grid=(frames,),
        in_specs=[smem_spec, smem_spec] + [any_spec] * (3 * strips) + [whole(probe_modes), whole(kern)] + tab_specs,
        out_specs=[per_frame(*wave_shape), per_frame(*pair_shape)],
        out_shape=[
            jax.ShapeDtypeStruct((frames,) + wave_shape, F32),
            jax.ShapeDtypeStruct((frames,) + pair_shape, F32),
        ],
        scratch_shapes=[ext, sems],
        compiler_params=params,
        cost_estimate=cost,
        name="forward_waves",
    )(all_positions, side, *first, probe_modes, kern, *tabs)

    back, core1, above1, below1 = pl.pallas_call(
        functools.partial(middle_kernel, strips, modes),
        grid=(frames,),
        in_specs=[smem_spec, smem_spec]
        + [any_spec] * (3 * strips)
        + [per_frame(*wave_shape), whole(level), per_frame(length, length)]
        + tab_specs,
        out_specs=[per_frame(*wave_shape)] + [any_spec] * 3,
        out_shape=[jax.ShapeDtypeStruct((frames,) + wave_shape, F32)] + grads_out,
        scratch_shapes=[
            ext,
            ext,
            pltpu.VMEM(pair_shape, F32),
            pltpu.VMEM(wave_shape, F32),
            pltpu.VMEM(pair_shape, F32),
            pltpu.VMEM((length, length), F32),
            sems,
        ],
        compiler_params=params,
        cost_estimate=cost,
        name="far_field",
    )(all_positions, side, *second, waves, level, measured, *tabs)

    term, core0, above0, below0 = pl.pallas_call(
        functools.partial(backward_kernel, strips, modes),
        grid=(frames,),
        in_specs=[smem_spec, smem_spec, per_frame(*wave_shape), per_frame(*pair_shape), whole(probe_modes), whole(kern)]
        + tab_specs,
        out_specs=[pl.BlockSpec(wave_shape, lambda i: (0, 0, 0, 0))] + [any_spec] * 3,
        out_shape=[jax.ShapeDtypeStruct(wave_shape, F32)] + grads_out,
        scratch_shapes=[ext, pltpu.VMEM(pair_shape, F32), sems],
        compiler_params=params,
        cost_estimate=cost,
        name="backward_waves",
    )(all_positions, side, back, windows, probe_modes, kern, *tabs)

    in_middle = (place == low) | (place == high)

    def folded(core, above, below, part):
        lower = tile_shift(above[part], -1)
        upper = tile_shift(below[part], 1)
        return core[part] + jnp.concatenate([upper, lower], axis=2)

    def scattered(core, above, below):
        far = folded(core, above, below, slice(half, strips))
        sent = [across(far[k]) for k in reversed(range(half))][::-1]
        near = folded(core, above, below, slice(0, half))
        total = [near[k] + sent[k] for k in range(half)]
        out = jnp.where(in_middle, total[0], 0.0)
        for k in range(1, half):
            out = out + lax.ppermute(total[k], "frame", [(low, low - k), (high, high + k)])
        return out

    grad1 = scattered(core1, above1, below1)
    grad0 = scattered(core0, above0, below0)
    object_grad = jnp.stack([grad0, grad1])

    count = lax.axis_size("tile")
    tile_at = lax.axis_index("tile")
    bits = []
    while 1 << len(bits) < count:
        bits.append(1 << len(bits))
    piece = jnp.where(in_middle, term.reshape(-1, length), 0.0)
    for bit in bits:
        size = piece.shape[0] // 2
        upper = (tile_at & bit) != 0
        first_half, second_half = piece[:size], piece[size:]
        piece = jnp.where(upper, second_half, first_half) + tile_swap(
            jnp.where(upper, first_half, second_half), bit
        )
    piece = piece + across(piece)
    spread = piece
    for k in range(1, half):
        spread = spread + lax.ppermute(piece, "frame", [(low, low - k), (high, high + k)])
    for bit in reversed(bits):
        upper = (tile_at & bit) != 0
        received = tile_swap(spread, bit)
        spread = jnp.concatenate(
            [jnp.where(upper, received, spread), jnp.where(upper, spread, received)], axis=0
        )
    probe_grad = spread.reshape(probe_modes.shape)
    return (object_grad, probe_grad)


def solution(mesh):
    in_specs = (
        P(None, None, "tile", "frame"),
        P(),
        P(),
        P(),
        P(("tile", "frame"), None),
        P(("tile", "frame"), None, None),
    )
    out_specs = (P(None, None, "tile", "frame"), P())
    return jax.shard_map(shards, mesh=mesh, in_specs=in_specs, out_specs=out_specs, check_vma=False)
```
